32 devices in a mesh: rows: 8 (over z, core), cols: 4 (over y, x).
Axes of the slice: x: 2, y: 2, z: 4, core: 2. Of those that a mesh axis runs over, the one named last changes fastest.
Arguments:
- wave_coarse: float32 [192, 192, 192], P('rows', 'cols'), may hold values from -6 to 6
- potential_coarse: float32 [192, 192, 192], P('rows', 'cols'), may hold values from 0 to 5
- potential_fine: float32 [384, 384, 384], P('cols', 'rows'), may hold values from 0 to 5
Outputs:
- fine_wave: float32 [384, 384, 384], P('cols', 'rows')
The draws below stay inside these ranges and needn't reach their ends.
All inputs are finite; a program needn't handle non-finite values.
Results may differ from the reference program's by a relative error of at most 0.0003.
Values sent between devices are 32-bit elements; how exact they have to be, the bound alone decides.
A program may use at most 128 MiB of HBM per device.

```python
import math
import jax
import jax.numpy as jnp
from jax import lax

NC = 192
NF = 384
COARSE_STEPS = 1
FINE_STEPS = 1


def incline_potential(key, length, steepness, rough_low, rough_high):
    positions = jnp.arange(length, dtype=jnp.float32) / length
    incline = steepness * (positions[:, None, None] + positions[None, :, None] + positions[None, None, :])
    roughness = jax.random.uniform(key, (length, length, length), jnp.float32, rough_low, rough_high)
    return incline + roughness


def draw_potential_coarse(key, part):
    return incline_potential(jax.random.fold_in(key, 11), NC, 1.1, 0.0, 1.5)


def draw_potential_fine(key, part):
    return incline_potential(jax.random.fold_in(key, 23), NF, 1.1, 0.0, 1.5)


def steps_of(rng, extent, shards, least, top_value):
    loudness = 1.0
    for position, blocks in shards:
        draws = jax.random.uniform(jax.random.fold_in(jax.random.fold_in(rng, 6), position), (blocks,), jnp.float32, least / len(shards), top_value / len(shards))
        loudness = loudness * jnp.repeat(jnp.exp(draws), extent[position] // blocks).reshape((-1,) + (1,) * (len(extent) - 1 - position))
    return loudness


def scatter_about(key, dims, scale, reach, shards=(), kind=jnp.bfloat16):
    gain = steps_of(key, dims, shards, -0.22, 0.18) if shards else 1.0
    drawn = jax.random.normal(key, dims, jnp.float32) * scale * gain
    return jnp.minimum(jnp.maximum(drawn, -reach), reach).astype(kind)


def setup_inputs(seed: int = 0) -> dict:
    seeds = jax.random.split(jax.random.key(seed), 4)
    return {
        "wave_coarse": scatter_about(seeds[0], (NC, NC, NC), 1.0, 6.0, ((0, 8), (1, 4)), jnp.float32),
        "potential_coarse": draw_potential_coarse(jax.random.fold_in(seeds[3], 71), 0),
        "potential_fine": draw_potential_fine(jax.random.fold_in(seeds[3], 71), 0),
    }


TIME_STEP = 0.5
CONTACT = 0.4
DIPOLE_STRENGTH = 0.3
EPSILON = 1e-06

def hartley(values, dimension):
    spectrum = jnp.fft.fft(values, axis=dimension)
    return (spectrum.real - spectrum.imag).astype(values.dtype)

def hartley_cube(values):
    for dimension in range(3):
        values = hartley(values, dimension)
    return values

def wavenumbers(length, spacing):
    positions = jnp.arange(length, dtype=jnp.int32)
    signed = jnp.where(positions < length // 2, positions, positions - length)
    return 2.0 * math.pi / (length * spacing) * signed.astype(jnp.float32)

def multipliers(along_x, along_y, along_z, length):
    squares = along_x + along_y + along_z
    volume = float(length) ** 3
    kinetic = jnp.exp(-0.5 * TIME_STEP * squares) / volume
    nonzero = jnp.where(squares > 0, squares, 1.0)
    dipolar = jnp.where(squares > 0, DIPOLE_STRENGTH * (3.0 * along_z - squares) / nonzero, 0.0) / volume
    return (kinetic, dipolar)

def advance(amplitude, potential, kinetic, dipolar, length):
    evolved = hartley_cube(kinetic * hartley_cube(amplitude))
    density = evolved * evolved
    field_dd = hartley_cube(dipolar * hartley_cube(density))
    damped = jnp.exp(-TIME_STEP * (potential + CONTACT * density + field_dd)) * evolved
    squares = jnp.sum(damped * damped)
    return damped * lax.rsqrt(squares / float(length) ** 3 + EPSILON)

def refine(values, dimension):
    spectrum = hartley(values, dimension)
    lower_half, upper_half = jnp.split(spectrum, 2, axis=dimension)
    empty_band = jnp.zeros_like(lower_half)
    padded = jnp.concatenate([lower_half, empty_band, empty_band, upper_half], axis=dimension)
    return hartley(padded, dimension) / NC

def grid_kernels(length, spacing):
    waves = wavenumbers(length, spacing)
    squared = waves * waves
    return multipliers(squared[:, None, None], squared[None, :, None], squared[None, None, :], length)

def reference(wave_coarse, potential_coarse, potential_fine):
    kinetic, dipolar = grid_kernels(NC, 2.0)
    amplitude = wave_coarse
    for repeat in range(COARSE_STEPS):
        amplitude = advance(amplitude, potential_coarse, kinetic, dipolar, NC)
    for dimension in range(3):
        amplitude = refine(amplitude, dimension)
    potential = jnp.transpose(potential_fine, (2, 1, 0))
    kinetic, dipolar = grid_kernels(NF, 1.0)
    for repeat in range(FINE_STEPS):
        amplitude = advance(amplitude, potential, kinetic, dipolar, NF)
    return jnp.transpose(amplitude, (2, 1, 0))
```

```python
import functools
import math

import jax
import jax.numpy as jnp
from jax import lax
from jax.experimental import pallas as pl
from jax.experimental.pallas import tpu as pltpu
from jax.sharding import PartitionSpec as P

TIME_STEP = 0.5
CONTACT = 0.4
DIPOLE_STRENGTH = 0.3
EPSILON = 1e-06
HIGH = lax.Precision.HIGH
HIGHEST = lax.Precision.HIGHEST
MESH = pl.DeviceIdType.MESH


def cas_values(product, length):
    phases = 2.0 * math.pi / length * (product % length).astype(jnp.float32)
    return jnp.cos(phases) + jnp.sin(phases)


def cas_matrix(length):
    positions = jnp.arange(length, dtype=jnp.int32)
    return cas_values(positions[:, None] * positions[None, :], length)


def lift_matrix(length):
    positions = jnp.arange(length, dtype=jnp.int32)
    lifted = jnp.where(positions < length // 2, positions, positions + length)
    fine_points = jnp.arange(2 * length, dtype=jnp.int32)
    return cas_values(lifted[:, None] * fine_points[None, :], 2 * length)


def wavenumbers(length, block_count, offset, spacing):
    positions = offset + jnp.arange(block_count, dtype=jnp.int32)
    signed = jnp.where(positions < length // 2, positions, positions - length)
    return 2.0 * math.pi / (length * spacing) * signed.astype(jnp.float32)


def dipolar_weights(along_x, along_y, along_z, length):
    squares = along_x + along_y + along_z
    nonzero = jnp.where(squares > 0, squares, 1.0)
    weights = jnp.where(squares > 0, DIPOLE_STRENGTH * (3.0 * along_z - squares) / nonzero, 0.0)
    return weights / float(length) ** 3


def exchange_kernel(axes, sizes, *refs):
    count = len(axes)
    sources, targets = refs[:count], refs[count : 2 * count]
    send_sems, recv_sems, local_sems = refs[2 * count :]
    row, col = lax.axis_index("rows"), lax.axis_index("cols")

    def place(axis, index):
        return (index, col) if axis == "rows" else (row, index)

    barrier = pltpu.get_barrier_semaphore()
    waits = 0
    for axis in sorted(set(axes)):
        size = sizes[axis]
        me = lax.axis_index(axis)
        for step in range(1, size):
            peer = lax.rem(me + step, size)
            pl.semaphore_signal(barrier, inc=1, device_id=place(axis, peer), device_id_type=MESH)
        waits += size - 1
    pl.semaphore_wait(barrier, waits)
    most = max(sizes[axis] for axis in axes)
    order = sorted(range(1, most), key=lambda step: abs(2 * step - most))
    copies = []
    for step in order:
        for index, axis in enumerate(axes):
            size = sizes[axis]
            if step >= size:
                continue
            me = lax.axis_index(axis)
            peer = lax.rem(me + step, size)
            copy = pltpu.make_async_remote_copy(
                src_ref=sources[index].at[peer],
                dst_ref=targets[index].at[me],
                send_sem=send_sems.at[index, step],
                recv_sem=recv_sems.at[index, step],
                device_id=place(axis, peer),
                device_id_type=MESH,
            )
            copy.start()
            copies.append(copy)
    for index, axis in enumerate(axes):
        me = lax.axis_index(axis)
        copy = pltpu.make_async_copy(
            sources[index].at[me], targets[index].at[me], local_sems.at[index]
        )
        copy.start()
        copies.append(copy)
    for copy in copies:
        copy.wait()


class Exchanger:
    def __init__(self, sizes):
        self.sizes = sizes
        self.calls = 0

    def __call__(self, *pairs):
        arrays = [array for array, _ in pairs]
        axes = tuple(axis for _, axis in pairs)
        most = max(self.sizes.values())
        count = len(arrays)
        self.calls += 1
        return pl.pallas_call(
            functools.partial(exchange_kernel, axes, self.sizes),
            out_shape=[jax.ShapeDtypeStruct(a.shape, a.dtype) for a in arrays],
            in_specs=[pl.BlockSpec(memory_space=pl.ANY)] * count,
            out_specs=[pl.BlockSpec(memory_space=pl.ANY)] * count,
            scratch_shapes=[
                pltpu.SemaphoreType.DMA((count, most)),
                pltpu.SemaphoreType.DMA((count, most)),
                pltpu.SemaphoreType.DMA((count,)),
            ],
            compiler_params=pltpu.CompilerParams(
                collective_id=self.calls - 1, has_side_effects=True
            ),
            name=f"exchange_{self.calls - 1}",
        )(*arrays)


def give(values, matrix, parts, precision=HIGH):
    if matrix is None:
        turned = jnp.transpose(values, (2, 0, 1))
    else:
        turned = jnp.einsum("abl,lk->kab", values, matrix, precision=precision)
    length, rows_extent, cols_extent = turned.shape
    return turned.reshape(parts, length // parts, rows_extent * cols_extent)


def take(received, axis, rows_extent):
    parts, block, area = received.shape
    cols_extent = area // rows_extent
    received = received.reshape(parts, block, rows_extent, cols_extent)
    if axis == "cols":
        return received.transpose(2, 1, 0, 3).reshape(rows_extent, block, parts * cols_extent)
    return received.transpose(1, 3, 0, 2).reshape(block, cols_extent, parts * rows_extent)


def apply(values, matrix, precision=HIGH):
    return jnp.einsum("abl,lk->abk", values, matrix, precision=precision)


def per_device(sizes, wave_coarse, potential_coarse, potential_fine):
    row, col = lax.axis_index("rows"), lax.axis_index("cols")
    rows, cols = sizes["rows"], sizes["cols"]
    nc, nf = wave_coarse.shape[2], potential_fine.shape[2]
    exchange = Exchanger(sizes)

    coarse_matrix = cas_matrix(nc)
    fine_matrix = cas_matrix(nf)
    decay = jnp.exp(-0.5 * TIME_STEP * wavenumbers(nc, nc, 0, 2.0) ** 2)[:, None] / nc
    evolve = jnp.dot(coarse_matrix, decay * coarse_matrix, precision=HIGHEST)
    lift = jnp.dot(coarse_matrix, decay * lift_matrix(nc), precision=HIGHEST)

    xr, yr, zr = nc // rows, nc // rows, nc // rows
    (got,) = exchange((give(wave_coarse, evolve, cols), "cols"))
    held = take(got, "cols", xr)
    (got,) = exchange((give(held, evolve, rows), "rows"))
    evolved = apply(take(got, "rows", xr), evolve)
    got, back = exchange(
        (give(evolved * evolved, coarse_matrix, cols), "cols"), (give(evolved, None, rows), "rows")
    )
    held, back = take(got, "cols", yr), take(back, "rows", yr)
    got, back = exchange(
        (give(held, coarse_matrix, rows), "rows"), (give(back, None, cols), "cols")
    )
    spectrum, evolved = take(got, "rows", yr), take(back, "cols", xr)
    z_block, x_block = nc // rows, nc // cols
    weights = dipolar_weights(
        wavenumbers(nc, x_block, col * x_block, 2.0)[None, :, None] ** 2,
        wavenumbers(nc, nc, 0, 2.0)[None, None, :] ** 2,
        wavenumbers(nc, z_block, row * z_block, 2.0)[:, None, None] ** 2,
        nc,
    )
    spectrum = weights * apply(spectrum, coarse_matrix)
    (got,) = exchange((give(spectrum, coarse_matrix, cols), "cols"))
    (got,) = exchange((give(take(got, "cols", zr), coarse_matrix, rows), "rows"))
    field_dd = apply(take(got, "rows", zr), coarse_matrix)
    density = evolved * evolved
    damped = jnp.exp(-TIME_STEP * (potential_coarse + CONTACT * density + field_dd)) * evolved
    partial_sum = jnp.sum(damped * damped)

    got, sums = exchange(
        (give(damped, lift, cols), "cols"),
        (jnp.full((cols, 8, 128), partial_sum, jnp.float32), "cols"),
    )
    partial_sum = jnp.sum(sums[:, 0, 0])
    got, sums = exchange(
        (give(take(got, "cols", xr), lift, rows), "rows"),
        (jnp.full((rows, 8, 128), partial_sum, jnp.float32), "rows"),
    )
    scale = lax.rsqrt(jnp.sum(sums[:, 0, 0]) / float(nc) ** 3 + EPSILON)
    evolved = jnp.einsum("abl,lk->bak", take(got, "rows", xr), lift, precision=HIGH) * scale

    density = evolved * evolved
    near, far = fine_matrix[:, : nf // 2], fine_matrix[:, nf // 2 :]
    swapped = density.transpose(1, 0, 2)
    yr = nf // rows
    got_near, got_far = exchange(
        (give(swapped, near, rows), "rows"), (give(swapped, far, cols), "cols")
    )
    near_field, far_field = take(got_near, "rows", yr), take(got_far, "cols", yr)
    near_rows = near_field.shape[0]
    got_near, got_far = exchange(
        (give(near_field, fine_matrix, cols), "cols"), (give(far_field, fine_matrix, rows), "rows")
    )
    near_field = apply(take(got_near, "cols", near_rows), fine_matrix)
    far_field = apply(take(got_far, "rows", yr), fine_matrix)
    y_block, z_block = nf // cols, nf // rows
    near_cols = nf // 2 // rows
    far_cols = nf // 2 // cols
    every = wavenumbers(nf, nf, 0, 1.0)[None, None, :] ** 2
    near_field = near_field * dipolar_weights(
        wavenumbers(nf, near_cols, row * near_cols, 1.0)[:, None, None] ** 2,
        wavenumbers(nf, y_block, col * y_block, 1.0)[None, :, None] ** 2,
        every,
        nf,
    )
    far_field = far_field * dipolar_weights(
        wavenumbers(nf, far_cols, nf // 2 + col * far_cols, 1.0)[None, :, None] ** 2,
        every,
        wavenumbers(nf, z_block, row * z_block, 1.0)[:, None, None] ** 2,
        nf,
    )
    got_near, got_far = exchange(
        (give(near_field, fine_matrix, cols), "cols"), (give(far_field, fine_matrix, rows), "rows")
    )
    near_field, far_field = take(got_near, "cols", near_rows), take(got_far, "rows", z_block)
    got_near, got_far = exchange(
        (give(near_field, fine_matrix, rows), "rows"), (give(far_field, fine_matrix, cols), "cols")
    )
    near_field, far_field = take(got_near, "rows", near_rows), take(got_far, "cols", yr)
    spectrum = jnp.concatenate([near_field, far_field], axis=2)
    field_dd = jnp.einsum("abl,lk->bak", spectrum, fine_matrix, precision=HIGH)
    damped = jnp.exp(-TIME_STEP * (potential_fine + CONTACT * density + field_dd)) * evolved
    total = jnp.sum(damped * damped)
    for axis in ("rows", "cols"):
        (sums,) = exchange((jnp.full((sizes[axis], 8, 128), total, jnp.float32), axis))
        total = jnp.sum(sums[:, 0, 0])
    return damped * lax.rsqrt(total / float(nf) ** 3 + EPSILON)


def solution(mesh):
    sizes = {"rows": mesh.shape["rows"], "cols": mesh.shape["cols"]}
    placed = (P("rows", "cols", None), P("rows", "cols", None), P("cols", "rows", None))
    return jax.shard_map(
        functools.partial(per_device, sizes),
        mesh=mesh,
        in_specs=placed,
        out_specs=P("cols", "rows", None),
        check_vma=False,
    )
```

```python
import functools
import math

import jax
import jax.numpy as jnp
from jax import lax
from jax.experimental import pallas as pl
from jax.experimental.pallas import tpu as pltpu
from jax.sharding import PartitionSpec as P

TIME_STEP = 0.5
CONTACT = 0.4
DIPOLE_STRENGTH = 0.3
EPSILON = 1e-06
HIGH = lax.Precision.HIGH
HIGHEST = lax.Precision.HIGHEST
MESH = pl.DeviceIdType.MESH


def cas_values(product, length):
    phases = 2.0 * math.pi / length * (product % length).astype(jnp.float32)
    return jnp.cos(phases) + jnp.sin(phases)


def cas_matrix(length):
    positions = jnp.arange(length, dtype=jnp.int32)
    return cas_values(positions[:, None] * positions[None, :], length)


def lift_matrix(length):
    positions = jnp.arange(length, dtype=jnp.int32)
    lifted = jnp.where(positions < length // 2, positions, positions + length)
    fine_points = jnp.arange(2 * length, dtype=jnp.int32)
    return cas_values(lifted[:, None] * fine_points[None, :], 2 * length)


def wavenumbers(length, block_count, offset, spacing):
    positions = offset + jnp.arange(block_count, dtype=jnp.int32)
    signed = jnp.where(positions < length // 2, positions, positions - length)
    return 2.0 * math.pi / (length * spacing) * signed.astype(jnp.float32)


def dipolar_weights(along_x, along_y, along_z, length):
    squares = along_x + along_y + along_z
    nonzero = jnp.where(squares > 0, squares, 1.0)
    weights = jnp.where(squares > 0, DIPOLE_STRENGTH * (3.0 * along_z - squares) / nonzero, 0.0)
    return weights / float(length) ** 3


def exchange_kernel(axes, sizes, *refs):
    count = len(axes)
    sources, targets = refs[:count], refs[count : 2 * count]
    send_sems, recv_sems, local_sems = refs[2 * count :]
    row, col = lax.axis_index("rows"), lax.axis_index("cols")

    def place(axis, index):
        return (index, col) if axis == "rows" else (row, index)

    barrier = pltpu.get_barrier_semaphore()
    waits = 0
    for axis in sorted(set(axes)):
        size = sizes[axis]
        me = lax.axis_index(axis)
        for step in range(1, size):
            peer = lax.rem(me + step, size)
            pl.semaphore_signal(barrier, inc=1, device_id=place(axis, peer), device_id_type=MESH)
        waits += size - 1
    pl.semaphore_wait(barrier, waits)
    most = max(sizes[axis] for axis in axes)
    order = sorted(range(1, most), key=lambda step: abs(2 * step - most))
    copies = []
    for step in order:
        for index, axis in enumerate(axes):
            size = sizes[axis]
            if step >= size:
                continue
            me = lax.axis_index(axis)
            peer = lax.rem(me + step, size)
            copy = pltpu.make_async_remote_copy(
                src_ref=sources[index].at[peer],
                dst_ref=targets[index].at[me],
                send_sem=send_sems.at[index, step],
                recv_sem=recv_sems.at[index, step],
                device_id=place(axis, peer),
                device_id_type=MESH,
            )
            copy.start()
            copies.append(copy)
    for index, axis in enumerate(axes):
        me = lax.axis_index(axis)
        copy = pltpu.make_async_copy(
            sources[index].at[me], targets[index].at[me], local_sems.at[index]
        )
        copy.start()
        copies.append(copy)
    for copy in copies:
        copy.wait()


class Exchanger:
    def __init__(self, sizes):
        self.sizes = sizes
        self.calls = 0

    def __call__(self, *pairs):
        arrays = [array for array, _ in pairs]
        axes = tuple(axis for _, axis in pairs)
        most = max(self.sizes.values())
        count = len(arrays)
        self.calls += 1
        return pl.pallas_call(
            functools.partial(exchange_kernel, axes, self.sizes),
            out_shape=[jax.ShapeDtypeStruct(a.shape, a.dtype) for a in arrays],
            in_specs=[pl.BlockSpec(memory_space=pl.ANY)] * count,
            out_specs=[pl.BlockSpec(memory_space=pl.ANY)] * count,
            scratch_shapes=[
                pltpu.SemaphoreType.DMA((count, most)),
                pltpu.SemaphoreType.DMA((count, most)),
                pltpu.SemaphoreType.DMA((count,)),
            ],
            compiler_params=pltpu.CompilerParams(
                collective_id=self.calls - 1, has_side_effects=True
            ),
            name=f"exchange_{self.calls - 1}",
        )(*arrays)


def give(values, matrix, parts, precision=HIGH):
    if matrix is None:
        turned = jnp.transpose(values, (2, 0, 1))
    else:
        turned = jnp.einsum("abl,lk->kab", values, matrix, precision=precision)
    length, rows_extent, cols_extent = turned.shape
    return turned.reshape(parts, length // parts, rows_extent * cols_extent)


def take(received, axis, rows_extent):
    parts, block, area = received.shape
    cols_extent = area // rows_extent
    received = received.reshape(parts, block, rows_extent, cols_extent)
    if axis == "cols":
        return received.transpose(2, 1, 0, 3).reshape(rows_extent, block, parts * cols_extent)
    return received.transpose(1, 3, 0, 2).reshape(block, cols_extent, parts * rows_extent)


def apply(values, matrix, precision=HIGH):
    return jnp.einsum("abl,lk->abk", values, matrix, precision=precision)


def split_product(values, matrix):
    high = matrix.astype(jnp.bfloat16)
    low = (matrix - high.astype(jnp.float32)).astype(jnp.bfloat16)
    top = values.astype(jnp.bfloat16)
    rest = (values - top.astype(jnp.float32)).astype(jnp.bfloat16)
    product = functools.partial(jnp.dot, preferred_element_type=jnp.float32)
    return product(top, high) + (product(top, low) + product(rest, high))


def gather_pieces(received, held):
    parts, chunk = received.shape[0], held.shape[0]
    width = received.shape[2] // chunk
    for s in range(chunk):
        for p in range(parts):
            held[s, :, p * width : (p + 1) * width] = received[p, :, s * width : (s + 1) * width]


def scatter_pieces(held, sent):
    parts, chunk = sent.shape[0], held.shape[0]
    width = sent.shape[2] // chunk
    for s in range(chunk):
        for p in range(parts):
            sent[p, :, s * width : (s + 1) * width] = held[s, :, p * width : (p + 1) * width]


def assemble_kernel(received, matrix, out, held):
    gather_pieces(received, held)
    chunk, k, length = held.shape
    product = split_product(held[...].reshape(chunk * k, length), matrix[...])
    out[...] = product.reshape(out.shape)


def middle_kernel(vertical, volume, received, matrix, sq_s, sq_k, sq_l, sent, held):
    gather_pieces(received, held)
    chunk, k, length = held.shape
    values = split_product(held[...].reshape(chunk * k, length), matrix[...])
    parts = [sq_s[...], sq_k[...][None], sq_l[...][None]]
    parts = [jnp.broadcast_to(part, held.shape) for part in parts]
    squares = parts[0] + parts[1] + parts[2]
    nonzero = jnp.where(squares > 0, squares, 1.0)
    weights = jnp.where(
        squares > 0, DIPOLE_STRENGTH * (3.0 * parts[vertical] - squares) / nonzero, 0.0
    )
    values = values * (weights / volume).reshape(chunk * k, length)
    held[...] = split_product(values, matrix[...]).reshape(held.shape)
    scatter_pieces(held, sent)


def chunk_of(spectators, width, k):
    for chunk in range(1, spectators):
        if spectators % chunk == 0 and chunk * width % 128 == 0 and chunk * k >= 256:
            return chunk
    return spectators


def assemble(received, spectators, matrix):
    parts, k, area = received.shape
    chunk = chunk_of(spectators, area // spectators, k)
    length, points = matrix.shape
    return pl.pallas_call(
        assemble_kernel,
        grid=(spectators // chunk,),
        in_specs=[
            pl.BlockSpec((parts, k, area // spectators * chunk), lambda i: (0, 0, i)),
            pl.BlockSpec((length, points), lambda i: (0, 0)),
        ],
        out_specs=pl.BlockSpec((chunk, k, points), lambda i: (i, 0, 0)),
        out_shape=jax.ShapeDtypeStruct((spectators, k, points), jnp.float32),
        scratch_shapes=[pltpu.VMEM((chunk, k, length), jnp.float32)],
    )(received, matrix)


def middle(received, matrix, sq_s, sq_k, sq_l, vertical):
    parts, k, area = received.shape
    spectators, length = sq_s.shape[0], matrix.shape[0]
    chunk = chunk_of(spectators, area // spectators, k)
    block = pl.BlockSpec((parts, k, area // spectators * chunk), lambda i: (0, 0, i))
    return pl.pallas_call(
        functools.partial(middle_kernel, vertical, float(length) ** 3),
        grid=(spectators // chunk,),
        in_specs=[
            block,
            pl.BlockSpec((length, length), lambda i: (0, 0)),
            pl.BlockSpec((chunk, 1, 1), lambda i: (i, 0, 0)),
            pl.BlockSpec((k, 1), lambda i: (0, 0)),
            pl.BlockSpec((1, length), lambda i: (0, 0)),
        ],
        out_specs=block,
        out_shape=jax.ShapeDtypeStruct(received.shape, jnp.float32),
        scratch_shapes=[pltpu.VMEM((chunk, k, length), jnp.float32)],
    )(received, matrix, sq_s[:, None, None], sq_k[:, None], sq_l[None, :])


def blocks(turned, parts):
    first, length, last = turned.shape
    turned = turned.reshape(first, parts, length // parts, last).transpose(1, 0, 2, 3)
    return turned.reshape(parts, first, length // parts * last)


def product_blocks(matrix, received, parts):
    turned = jnp.dot(matrix, received.reshape(-1, received.shape[2]), precision=HIGH)
    return turned.reshape(parts, turned.shape[0] // parts, turned.shape[1])


def per_device(sizes, wave_coarse, potential_coarse, potential_fine):
    row, col = lax.axis_index("rows"), lax.axis_index("cols")
    rows, cols = sizes["rows"], sizes["cols"]
    nc, nf = wave_coarse.shape[2], potential_fine.shape[2]
    exchange = Exchanger(sizes)

    coarse_matrix = cas_matrix(nc)
    fine_matrix = cas_matrix(nf)
    decay = jnp.exp(-0.5 * TIME_STEP * wavenumbers(nc, nc, 0, 2.0) ** 2)[:, None] / nc
    evolve = jnp.dot(coarse_matrix, decay * coarse_matrix, precision=HIGHEST)
    lift = jnp.dot(coarse_matrix, decay * lift_matrix(nc), precision=HIGHEST)

    xr, yr, zr = nc // rows, nc // rows, nc // rows
    (got,) = exchange((give(wave_coarse, evolve, cols), "cols"))
    held = take(got, "cols", xr)
    (got,) = exchange((give(held, evolve, rows), "rows"))
    evolved = apply(take(got, "rows", xr), evolve)
    got, back = exchange(
        (give(evolved * evolved, coarse_matrix, cols), "cols"), (give(evolved, None, rows), "rows")
    )
    held, back = take(got, "cols", yr), take(back, "rows", yr)
    got, back = exchange(
        (give(held, coarse_matrix, rows), "rows"), (give(back, None, cols), "cols")
    )
    spectrum, evolved = take(got, "rows", yr), take(back, "cols", xr)
    z_block, x_block = nc // rows, nc // cols
    weights = dipolar_weights(
        wavenumbers(nc, x_block, col * x_block, 2.0)[None, :, None] ** 2,
        wavenumbers(nc, nc, 0, 2.0)[None, None, :] ** 2,
        wavenumbers(nc, z_block, row * z_block, 2.0)[:, None, None] ** 2,
        nc,
    )
    spectrum = weights * apply(spectrum, coarse_matrix)
    (got,) = exchange((give(spectrum, coarse_matrix, cols), "cols"))
    (got,) = exchange((give(take(got, "cols", zr), coarse_matrix, rows), "rows"))
    field_dd = apply(take(got, "rows", zr), coarse_matrix)
    density = evolved * evolved
    damped = jnp.exp(-TIME_STEP * (potential_coarse + CONTACT * density + field_dd)) * evolved
    partial_sum = jnp.sum(damped * damped)

    got, sums = exchange(
        (blocks(jnp.einsum("xyz,zk->ykx", damped, lift, precision=HIGH), cols), "cols"),
        (jnp.full((cols, 8, 128), partial_sum, jnp.float32), "cols"),
    )
    partial_sum = jnp.sum(sums[:, 0, 0])
    got, sums = exchange(
        (product_blocks(lift.T, got, rows), "rows"),
        (jnp.full((rows, 8, 128), partial_sum, jnp.float32), "rows"),
    )
    scale = lax.rsqrt(jnp.sum(sums[:, 0, 0]) / float(nc) ** 3 + EPSILON)
    evolved = assemble(got, nf // cols, lift) * scale

    density = evolved * evolved
    half = nf // 2
    near, far = fine_matrix[:, :half], fine_matrix[:, half:]
    got_near, got_far = exchange(
        (blocks(jnp.einsum("zyx,xk->ykz", density, near, precision=HIGH), rows), "rows"),
        (blocks(jnp.einsum("zyx,xk->zky", density, far, precision=HIGH), cols), "cols"),
    )
    got_near, got_far = exchange(
        (product_blocks(fine_matrix, got_near, cols), "cols"),
        (product_blocks(fine_matrix, got_far, rows), "rows"),
    )
    y_block, z_block = nf // cols, nf // rows
    near_block, far_block = half // rows, half // cols
    every = wavenumbers(nf, nf, 0, 1.0) ** 2
    got_near = middle(
        got_near,
        fine_matrix,
        wavenumbers(nf, near_block, row * near_block, 1.0) ** 2,
        wavenumbers(nf, y_block, col * y_block, 1.0) ** 2,
        every,
        2,
    )
    got_far = middle(
        got_far,
        fine_matrix,
        wavenumbers(nf, far_block, half + col * far_block, 1.0) ** 2,
        wavenumbers(nf, z_block, row * z_block, 1.0) ** 2,
        every,
        1,
    )
    got_near, got_far = exchange((got_near, "cols"), (got_far, "rows"))
    got_near, got_far = exchange(
        (product_blocks(fine_matrix, got_near, rows), "rows"),
        (product_blocks(fine_matrix, got_far, cols), "cols"),
    )
    z_extent, y_extent = nf // cols, nf // rows
    near_field = got_near.reshape(rows, y_extent, near_block, z_extent)
    near_field = near_field.transpose(3, 1, 0, 2).reshape(z_extent, y_extent, half)
    far_field = got_far.reshape(cols, z_extent, far_block, y_extent)
    far_field = far_field.transpose(1, 3, 0, 2).reshape(z_extent, y_extent, half)
    spectrum = jnp.concatenate([near_field, far_field], axis=2)
    field_dd = jnp.einsum("zyk,kx->zyx", spectrum, fine_matrix, precision=HIGH)
    damped = jnp.exp(-TIME_STEP * (potential_fine + CONTACT * density + field_dd)) * evolved
    total = jnp.sum(damped * damped)
    for axis in ("rows", "cols"):
        (sums,) = exchange((jnp.full((sizes[axis], 8, 128), total, jnp.float32), axis))
        total = jnp.sum(sums[:, 0, 0])
    return damped * lax.rsqrt(total / float(nf) ** 3 + EPSILON)


def solution(mesh):
    sizes = {"rows": mesh.shape["rows"], "cols": mesh.shape["cols"]}
    placed = (P("rows", "cols", None), P("rows", "cols", None), P("cols", "rows", None))
    return jax.shard_map(
        functools.partial(per_device, sizes),
        mesh=mesh,
        in_specs=placed,
        out_specs=P("cols", "rows", None),
        check_vma=False,
    )
```

```python
import functools
import math

import jax
import jax.numpy as jnp
from jax import lax
from jax.experimental import pallas as pl
from jax.experimental.pallas import tpu as pltpu
from jax.sharding import PartitionSpec as P

TIME_STEP = 0.5
CONTACT = 0.4
DIPOLE_STRENGTH = 0.3
EPSILON = 1e-06
HIGH = lax.Precision.HIGH
HIGHEST = lax.Precision.HIGHEST
MESH = pl.DeviceIdType.MESH


def cas_values(product, length):
    phases = 2.0 * math.pi / length * (product % length).astype(jnp.float32)
    return jnp.cos(phases) + jnp.sin(phases)


def cas_matrix(length):
    positions = jnp.arange(length, dtype=jnp.int32)
    return cas_values(positions[:, None] * positions[None, :], length)


def lift_matrix(length):
    positions = jnp.arange(length, dtype=jnp.int32)
    lifted = jnp.where(positions < length // 2, positions, positions + length)
    fine_points = jnp.arange(2 * length, dtype=jnp.int32)
    return cas_values(lifted[:, None] * fine_points[None, :], 2 * length)


def wavenumbers(length, block_count, offset, spacing):
    positions = offset + jnp.arange(block_count, dtype=jnp.int32)
    signed = jnp.where(positions < length // 2, positions, positions - length)
    return 2.0 * math.pi / (length * spacing) * signed.astype(jnp.float32)


def dipolar_weights(along_x, along_y, along_z, length):
    squares = along_x + along_y + along_z
    nonzero = jnp.where(squares > 0, squares, 1.0)
    weights = jnp.where(squares > 0, DIPOLE_STRENGTH * (3.0 * along_z - squares) / nonzero, 0.0)
    return weights / float(length) ** 3


def exchange_kernel(axes, sizes, *refs):
    count = len(axes)
    sources, targets = refs[:count], refs[count : 2 * count]
    send_sems, recv_sems, local_sems = refs[2 * count :]
    row, col = lax.axis_index("rows"), lax.axis_index("cols")

    def place(axis, index):
        return (index, col) if axis == "rows" else (row, index)

    barrier = pltpu.get_barrier_semaphore()
    waits = 0
    for axis in sorted(set(axes)):
        size = sizes[axis]
        me = lax.axis_index(axis)
        for step in range(1, size):
            peer = lax.rem(me + step, size)
            pl.semaphore_signal(barrier, inc=1, device_id=place(axis, peer), device_id_type=MESH)
        waits += size - 1
    pl.semaphore_wait(barrier, waits)
    most = max(sizes[axis] for axis in axes)
    order = sorted(range(1, most), key=lambda step: abs(2 * step - most))
    copies = []
    for step in order:
        for index, axis in enumerate(axes):
            size = sizes[axis]
            if step >= size:
                continue
            me = lax.axis_index(axis)
            peer = lax.rem(me + step, size)
            copy = pltpu.make_async_remote_copy(
                src_ref=sources[index].at[peer],
                dst_ref=targets[index].at[me],
                send_sem=send_sems.at[index, step],
                recv_sem=recv_sems.at[index, step],
                device_id=place(axis, peer),
                device_id_type=MESH,
            )
            copy.start()
            copies.append(copy)
    for index, axis in enumerate(axes):
        me = lax.axis_index(axis)
        copy = pltpu.make_async_copy(
            sources[index].at[me], targets[index].at[me], local_sems.at[index]
        )
        copy.start()
        copies.append(copy)
    for copy in copies:
        copy.wait()


class Exchanger:
    def __init__(self, sizes):
        self.sizes = sizes
        self.calls = 0

    def __call__(self, *pairs):
        arrays = [array for array, _ in pairs]
        axes = tuple(axis for _, axis in pairs)
        most = max(self.sizes.values())
        count = len(arrays)
        self.calls += 1
        return pl.pallas_call(
            functools.partial(exchange_kernel, axes, self.sizes),
            out_shape=[jax.ShapeDtypeStruct(a.shape, a.dtype) for a in arrays],
            in_specs=[pl.BlockSpec(memory_space=pl.ANY)] * count,
            out_specs=[pl.BlockSpec(memory_space=pl.ANY)] * count,
            scratch_shapes=[
                pltpu.SemaphoreType.DMA((count, most)),
                pltpu.SemaphoreType.DMA((count, most)),
                pltpu.SemaphoreType.DMA((count,)),
            ],
            compiler_params=pltpu.CompilerParams(
                collective_id=self.calls - 1, has_side_effects=True
            ),
            name=f"exchange_{self.calls - 1}",
        )(*arrays)


def give(values, matrix, parts, precision=HIGH):
    if matrix is None:
        turned = jnp.transpose(values, (2, 0, 1))
    else:
        turned = jnp.einsum("abl,lk->kab", values, matrix, precision=precision)
    length, rows_extent, cols_extent = turned.shape
    return turned.reshape(parts, length // parts, rows_extent * cols_extent)


def take(received, axis, rows_extent):
    parts, block, area = received.shape
    cols_extent = area // rows_extent
    received = received.reshape(parts, block, rows_extent, cols_extent)
    if axis == "cols":
        return received.transpose(2, 1, 0, 3).reshape(rows_extent, block, parts * cols_extent)
    return received.transpose(1, 3, 0, 2).reshape(block, cols_extent, parts * rows_extent)


def apply(values, matrix, precision=HIGH):
    return jnp.einsum("abl,lk->abk", values, matrix, precision=precision)


def split_product(values, matrix):
    high = matrix.astype(jnp.bfloat16)
    low = (matrix - high.astype(jnp.float32)).astype(jnp.bfloat16)
    top = values.astype(jnp.bfloat16)
    rest = (values - top.astype(jnp.float32)).astype(jnp.bfloat16)
    product = functools.partial(jnp.dot, preferred_element_type=jnp.float32)
    return product(top, high) + (product(top, low) + product(rest, high))


def gather_pieces(received, held):
    parts, chunk = received.shape[0], held.shape[0]
    width = received.shape[2] // chunk
    for s in range(chunk):
        for p in range(parts):
            held[s, :, p * width : (p + 1) * width] = received[p, :, s * width : (s + 1) * width]


def scatter_pieces(held, sent):
    parts, chunk = sent.shape[0], held.shape[0]
    width = sent.shape[2] // chunk
    for s in range(chunk):
        for p in range(parts):
            sent[p, :, s * width : (s + 1) * width] = held[s, :, p * width : (p + 1) * width]


def assemble_kernel(received, matrix, out, held):
    gather_pieces(received, held)
    chunk, k, length = held.shape
    product = split_product(held[...].reshape(chunk * k, length), matrix[...])
    out[...] = product.reshape(out.shape)


def chunk_of(spectators, width, k):
    for chunk in range(1, spectators):
        if spectators % chunk == 0 and chunk * width % 128 == 0 and chunk * k >= 256:
            return chunk
    return spectators


def assemble(received, spectators, matrix):
    parts, k, area = received.shape
    chunk = chunk_of(spectators, area // spectators, k)
    length, points = matrix.shape
    return pl.pallas_call(
        assemble_kernel,
        grid=(spectators // chunk,),
        in_specs=[
            pl.BlockSpec((parts, k, area // spectators * chunk), lambda i: (0, 0, i)),
            pl.BlockSpec((length, points), lambda i: (0, 0)),
        ],
        out_specs=pl.BlockSpec((chunk, k, points), lambda i: (i, 0, 0)),
        out_shape=jax.ShapeDtypeStruct((spectators, k, points), jnp.float32),
        scratch_shapes=[pltpu.VMEM((chunk, k, length), jnp.float32)],
    )(received, matrix)


def halves(values):
    high = values.astype(jnp.bfloat16)
    return high, (values - high.astype(jnp.float32)).astype(jnp.bfloat16)


def product_of(left, right):
    product = functools.partial(jnp.dot, preferred_element_type=jnp.float32)
    return product(left[0], right[0]) + (product(left[0], right[1]) + product(left[1], right[0]))


def planes_kernel(flows, sizes, chunks, volume, *refs):
    row, col = lax.axis_index("rows"), lax.axis_index("cols")

    def place(axis, index):
        return (index, col) if axis == "rows" else (row, index)

    matrix = refs[0]
    inputs = [refs[1 + 4 * i : 5 + 4 * i] for i in range(len(flows))]
    at = 1 + 4 * len(flows)
    outs = refs[at : at + len(flows)]
    at += len(flows)
    high, low = refs[at : at + 2]
    at += 2
    buffers = [refs[at + 9 * i : at + 9 * i + 9] for i in range(len(flows))]

    barrier = pltpu.get_barrier_semaphore()
    waits = 0
    for axis in sorted(set(axis for axis, _ in flows)):
        size = sizes[axis]
        me = lax.axis_index(axis)
        for step in range(1, size):
            peer = lax.rem(me + step, size)
            pl.semaphore_signal(barrier, inc=1, device_id=place(axis, peer), device_id_type=MESH)
        waits += size - 1
    high[...], low[...] = halves(matrix[...])
    pl.semaphore_wait(barrier, waits)

    def copies(flow, turn, c):
        axis, _ = flows[flow]
        size = sizes[axis]
        me = lax.axis_index(axis)
        sent, received = buffers[flow][2 * turn : 2 * turn + 2]
        send_sem, recv_sem = buffers[flow][4 + 2 * turn : 6 + 2 * turn]
        order = sorted(range(1, size), key=lambda step: abs(2 * step - size))
        for step in order:
            peer = lax.rem(me + step, size)
            yield pltpu.make_async_remote_copy(
                src_ref=sent.at[c, peer],
                dst_ref=received.at[c, me],
                send_sem=send_sem.at[c, step],
                recv_sem=recv_sem.at[c, step],
                device_id=place(axis, peer),
                device_id_type=MESH,
            )

    def launch(flow, turn, c):
        me = lax.axis_index(flows[flow][0])
        for copy in copies(flow, turn, c):
            copy.start()
        sent, received = buffers[flow][2 * turn : 2 * turn + 2]
        received[c, me] = sent[c, me]

    def lanes(area, c):
        if chunks == 1:
            return slice(None)
        return pl.ds(pl.multiple_of(c * (area // chunks), 128), area // chunks)

    def first(c, carry):
        for flow in range(len(flows)):
            source, sent = inputs[flow][0], buffers[flow][0]
            part = source[:, :, lanes(source.shape[2], c)]
            part = part.reshape(matrix.shape[0], part.shape[2])
            product = product_of((high[...], low[...]), halves(part))
            sent[c] = product.reshape(sent.shape[1:])
            launch(flow, 0, c)
        return carry

    def second(c, carry):
        for flow in range(len(flows)):
            _, sq_s, sq_k, sq_l = inputs[flow]
            vertical = flows[flow][1]
            held = buffers[flow][8]
            chunk, k, length = held.shape
            for copy in copies(flow, 0, c):
                copy.wait_recv()
            gather_pieces(buffers[flow][1].at[c], held)
            both = (high[...], low[...])
            values = product_of(halves(held[...].reshape(chunk * k, length)), both)
            parts = [sq_s[pl.ds(c * chunk, chunk)], sq_k[...][None], sq_l[...][None]]
            parts = [jnp.broadcast_to(part, held.shape) for part in parts]
            squares = parts[0] + parts[1] + parts[2]
            nonzero = jnp.where(squares > 0, squares, 1.0)
            weights = jnp.where(
                squares > 0, DIPOLE_STRENGTH * (3.0 * parts[vertical] - squares) / nonzero, 0.0
            )
            values = values * (weights / volume).reshape(chunk * k, length)
            held[...] = product_of(halves(values), both).reshape(held.shape)
            scatter_pieces(held, buffers[flow][2].at[c])
            launch(flow, 1, c)
        return carry

    def third(c, carry):
        for flow in range(len(flows)):
            for copy in copies(flow, 1, c):
                copy.wait_recv()
            received, out = buffers[flow][3], outs[flow]
            part = received[c].reshape(matrix.shape[0], received.shape[3])
            product = product_of((high[...], low[...]), halves(part))
            out[:, lanes(out.shape[1], c)] = product
            for turn in range(2):
                for copy in copies(flow, turn, c):
                    copy.wait_send()
        return carry

    for stage in (first, second, third):
        lax.fori_loop(0, chunks, stage, 0)


def planes(exchange, flows, matrix):
    sizes = exchange.sizes
    length = matrix.shape[0]
    counts = []
    for axis, _, received, sq_s, sq_k, _ in flows:
        spectators = sq_s.shape[0]
        width = received.shape[2] // spectators
        counts.append(spectators // chunk_of(spectators, width, sq_k.shape[0]))
    chunks = counts[0] if len(set(counts)) == 1 else 1
    operands, outs, scratch = [matrix], [], []
    scratch += [pltpu.VMEM((length, length), jnp.bfloat16)] * 2
    for axis, _, received, sq_s, sq_k, sq_l in flows:
        operands += [received, sq_s[:, None, None], sq_k[:, None], sq_l[None, :]]
        area, k, size = received.shape[2], sq_k.shape[0], sizes[axis]
        outs.append(jax.ShapeDtypeStruct((length, area), jnp.float32))
        scratch += [pltpu.VMEM((chunks, size, k, area // chunks), jnp.float32)] * 4
        scratch += [pltpu.SemaphoreType.DMA((chunks, size))] * 4
        scratch += [pltpu.VMEM((sq_s.shape[0] // chunks, k, length), jnp.float32)]
    exchange.calls += 1
    vmem = pl.BlockSpec(memory_space=pltpu.VMEM)
    return pl.pallas_call(
        functools.partial(
            planes_kernel,
            tuple((flow[0], flow[1]) for flow in flows),
            sizes,
            chunks,
            float(length) ** 3,
        ),
        out_shape=outs,
        in_specs=[vmem] * len(operands),
        out_specs=[vmem] * len(outs),
        scratch_shapes=scratch,
        compiler_params=pltpu.CompilerParams(
            collective_id=exchange.calls - 1,
            has_side_effects=True,
            vmem_limit_bytes=60 * 1024 * 1024,
        ),
        name=f"planes_{exchange.calls - 1}",
    )(*operands)


def blocks(turned, parts):
    first, length, last = turned.shape
    turned = turned.reshape(first, parts, length // parts, last).transpose(1, 0, 2, 3)
    return turned.reshape(parts, first, length // parts * last)


def product_blocks(matrix, received, parts):
    turned = jnp.dot(matrix, received.reshape(-1, received.shape[2]), precision=HIGH)
    return turned.reshape(parts, turned.shape[0] // parts, turned.shape[1])


def per_device(sizes, wave_coarse, potential_coarse, potential_fine):
    row, col = lax.axis_index("rows"), lax.axis_index("cols")
    rows, cols = sizes["rows"], sizes["cols"]
    nc, nf = wave_coarse.shape[2], potential_fine.shape[2]
    exchange = Exchanger(sizes)

    coarse_matrix = cas_matrix(nc)
    fine_matrix = cas_matrix(nf)
    decay = jnp.exp(-0.5 * TIME_STEP * wavenumbers(nc, nc, 0, 2.0) ** 2)[:, None] / nc
    evolve = jnp.dot(coarse_matrix, decay * coarse_matrix, precision=HIGHEST)
    lift = jnp.dot(coarse_matrix, decay * lift_matrix(nc), precision=HIGHEST)

    xr, yr, zr = nc // rows, nc // rows, nc // rows
    (got,) = exchange((give(wave_coarse, evolve, cols), "cols"))
    held = take(got, "cols", xr)
    (got,) = exchange((give(held, evolve, rows), "rows"))
    evolved = apply(take(got, "rows", xr), evolve)
    got, back = exchange(
        (give(evolved * evolved, coarse_matrix, cols), "cols"), (give(evolved, None, rows), "rows")
    )
    held, back = take(got, "cols", yr), take(back, "rows", yr)
    got, back = exchange(
        (give(held, coarse_matrix, rows), "rows"), (give(back, None, cols), "cols")
    )
    spectrum, evolved = take(got, "rows", yr), take(back, "cols", xr)
    z_block, x_block = nc // rows, nc // cols
    weights = dipolar_weights(
        wavenumbers(nc, x_block, col * x_block, 2.0)[None, :, None] ** 2,
        wavenumbers(nc, nc, 0, 2.0)[None, None, :] ** 2,
        wavenumbers(nc, z_block, row * z_block, 2.0)[:, None, None] ** 2,
        nc,
    )
    spectrum = weights * apply(spectrum, coarse_matrix)
    (got,) = exchange((give(spectrum, coarse_matrix, cols), "cols"))
    (got,) = exchange((give(take(got, "cols", zr), coarse_matrix, rows), "rows"))
    field_dd = apply(take(got, "rows", zr), coarse_matrix)
    density = evolved * evolved
    damped = jnp.exp(-TIME_STEP * (potential_coarse + CONTACT * density + field_dd)) * evolved
    partial_sum = jnp.sum(damped * damped)

    got, sums = exchange(
        (blocks(jnp.einsum("xyz,zk->ykx", damped, lift, precision=HIGH), cols), "cols"),
        (jnp.full((cols, 8, 128), partial_sum, jnp.float32), "cols"),
    )
    partial_sum = jnp.sum(sums[:, 0, 0])
    got, sums = exchange(
        (product_blocks(lift.T, got, rows), "rows"),
        (jnp.full((rows, 8, 128), partial_sum, jnp.float32), "rows"),
    )
    scale = lax.rsqrt(jnp.sum(sums[:, 0, 0]) / float(nc) ** 3 + EPSILON)
    evolved = assemble(got, nf // cols, lift) * scale

    density = evolved * evolved
    half = nf // 2
    near, far = fine_matrix[:, :half], fine_matrix[:, half:]
    got_near, got_far = exchange(
        (blocks(jnp.einsum("zyx,xk->ykz", density, near, precision=HIGH), rows), "rows"),
        (blocks(jnp.einsum("zyx,xk->zky", density, far, precision=HIGH), cols), "cols"),
    )
    y_block, z_block = nf // cols, nf // rows
    near_block, far_block = half // rows, half // cols
    every = wavenumbers(nf, nf, 0, 1.0) ** 2
    near_flow = (
        "cols",
        2,
        got_near,
        wavenumbers(nf, near_block, row * near_block, 1.0) ** 2,
        wavenumbers(nf, y_block, col * y_block, 1.0) ** 2,
        every,
    )
    far_flow = (
        "rows",
        1,
        got_far,
        wavenumbers(nf, far_block, half + col * far_block, 1.0) ** 2,
        wavenumbers(nf, z_block, row * z_block, 1.0) ** 2,
        every,
    )
    got_far, got_near = planes(exchange, (far_flow, near_flow), fine_matrix)
    got_near, got_far = exchange(
        (got_near.reshape(rows, nf // rows, -1), "rows"),
        (got_far.reshape(cols, nf // cols, -1), "cols"),
    )
    z_extent, y_extent = nf // cols, nf // rows
    near_field = got_near.reshape(rows, y_extent, near_block, z_extent)
    near_field = near_field.transpose(3, 1, 0, 2).reshape(z_extent, y_extent, half)
    far_field = got_far.reshape(cols, z_extent, far_block, y_extent)
    far_field = far_field.transpose(1, 3, 0, 2).reshape(z_extent, y_extent, half)
    spectrum = jnp.concatenate([near_field, far_field], axis=2)
    field_dd = jnp.einsum("zyk,kx->zyx", spectrum, fine_matrix, precision=HIGH)
    damped = jnp.exp(-TIME_STEP * (potential_fine + CONTACT * density + field_dd)) * evolved
    total = jnp.sum(damped * damped)
    for axis in ("rows", "cols"):
        (sums,) = exchange((jnp.full((sizes[axis], 8, 128), total, jnp.float32), axis))
        total = jnp.sum(sums[:, 0, 0])
    return damped * lax.rsqrt(total / float(nf) ** 3 + EPSILON)


def solution(mesh):
    sizes = {"rows": mesh.shape["rows"], "cols": mesh.shape["cols"]}
    placed = (P("rows", "cols", None), P("rows", "cols", None), P("cols", "rows", None))
    return jax.shard_map(
        functools.partial(per_device, sizes),
        mesh=mesh,
        in_specs=placed,
        out_specs=P("cols", "rows", None),
        check_vma=False,
    )
```

```python
import functools
import math

import jax
import jax.numpy as jnp
from jax import lax
from jax.experimental import pallas as pl
from jax.experimental.pallas import tpu as pltpu
from jax.sharding import PartitionSpec as P

TIME_STEP = 0.5
CONTACT = 0.4
DIPOLE_STRENGTH = 0.3
EPSILON = 1e-06
HIGH = lax.Precision.HIGH
HIGHEST = lax.Precision.HIGHEST
MESH = pl.DeviceIdType.MESH


def cas_values(product, length):
    phases = 2.0 * math.pi / length * (product % length).astype(jnp.float32)
    return jnp.cos(phases) + jnp.sin(phases)


def cas_matrix(length):
    positions = jnp.arange(length, dtype=jnp.int32)
    return cas_values(positions[:, None] * positions[None, :], length)


def lift_matrix(length):
    positions = jnp.arange(length, dtype=jnp.int32)
    lifted = jnp.where(positions < length // 2, positions, positions + length)
    fine_points = jnp.arange(2 * length, dtype=jnp.int32)
    return cas_values(lifted[:, None] * fine_points[None, :], 2 * length)


def wavenumbers(length, block_count, offset, spacing):
    positions = offset + jnp.arange(block_count, dtype=jnp.int32)
    signed = jnp.where(positions < length // 2, positions, positions - length)
    return 2.0 * math.pi / (length * spacing) * signed.astype(jnp.float32)


def dipolar_weights(along_x, along_y, along_z, length):
    squares = along_x + along_y + along_z
    nonzero = jnp.where(squares > 0, squares, 1.0)
    weights = jnp.where(squares > 0, DIPOLE_STRENGTH * (3.0 * along_z - squares) / nonzero, 0.0)
    return weights / float(length) ** 3


def exchange_kernel(axes, sizes, *refs):
    count = len(axes)
    sources, targets = refs[:count], refs[count : 2 * count]
    send_sems, recv_sems, local_sems = refs[2 * count :]
    row, col = lax.axis_index("rows"), lax.axis_index("cols")

    def place(axis, index):
        return (index, col) if axis == "rows" else (row, index)

    barrier = pltpu.get_barrier_semaphore()
    waits = 0
    for axis in sorted(set(axes)):
        size = sizes[axis]
        me = lax.axis_index(axis)
        for step in range(1, size):
            peer = lax.rem(me + step, size)
            pl.semaphore_signal(barrier, inc=1, device_id=place(axis, peer), device_id_type=MESH)
        waits += size - 1
    pl.semaphore_wait(barrier, waits)
    most = max(sizes[axis] for axis in axes)
    order = sorted(range(1, most), key=lambda step: abs(2 * step - most))
    copies = []
    for step in order:
        for index, axis in enumerate(axes):
            size = sizes[axis]
            if step >= size:
                continue
            me = lax.axis_index(axis)
            peer = lax.rem(me + step, size)
            copy = pltpu.make_async_remote_copy(
                src_ref=sources[index].at[peer],
                dst_ref=targets[index].at[me],
                send_sem=send_sems.at[index, step],
                recv_sem=recv_sems.at[index, step],
                device_id=place(axis, peer),
                device_id_type=MESH,
            )
            copy.start()
            copies.append(copy)
    for index, axis in enumerate(axes):
        me = lax.axis_index(axis)
        copy = pltpu.make_async_copy(
            sources[index].at[me], targets[index].at[me], local_sems.at[index]
        )
        copy.start()
        copies.append(copy)
    for copy in copies:
        copy.wait()


class Exchanger:
    def __init__(self, sizes):
        self.sizes = sizes
        self.calls = 0

    def __call__(self, *pairs):
        arrays = [array for array, _ in pairs]
        axes = tuple(axis for _, axis in pairs)
        most = max(self.sizes.values())
        count = len(arrays)
        self.calls += 1
        return pl.pallas_call(
            functools.partial(exchange_kernel, axes, self.sizes),
            out_shape=[jax.ShapeDtypeStruct(a.shape, a.dtype) for a in arrays],
            in_specs=[pl.BlockSpec(memory_space=pl.ANY)] * count,
            out_specs=[pl.BlockSpec(memory_space=pl.ANY)] * count,
            scratch_shapes=[
                pltpu.SemaphoreType.DMA((count, most)),
                pltpu.SemaphoreType.DMA((count, most)),
                pltpu.SemaphoreType.DMA((count,)),
            ],
            compiler_params=pltpu.CompilerParams(
                collective_id=self.calls - 1, has_side_effects=True
            ),
            name=f"exchange_{self.calls - 1}",
        )(*arrays)


def give(values, matrix, parts, precision=HIGH):
    if matrix is None:
        turned = jnp.transpose(values, (2, 0, 1))
    else:
        turned = jnp.einsum("abl,lk->kab", values, matrix, precision=precision)
    length, rows_extent, cols_extent = turned.shape
    return turned.reshape(parts, length // parts, rows_extent * cols_extent)


def take(received, axis, rows_extent):
    parts, block, area = received.shape
    cols_extent = area // rows_extent
    received = received.reshape(parts, block, rows_extent, cols_extent)
    if axis == "cols":
        return received.transpose(2, 1, 0, 3).reshape(rows_extent, block, parts * cols_extent)
    return received.transpose(1, 3, 0, 2).reshape(block, cols_extent, parts * rows_extent)


def apply(values, matrix, precision=HIGH):
    return jnp.einsum("abl,lk->abk", values, matrix, precision=precision)


def split_product(values, matrix):
    high = matrix.astype(jnp.bfloat16)
    low = (matrix - high.astype(jnp.float32)).astype(jnp.bfloat16)
    top = values.astype(jnp.bfloat16)
    rest = (values - top.astype(jnp.float32)).astype(jnp.bfloat16)
    product = functools.partial(jnp.dot, preferred_element_type=jnp.float32)
    return product(top, high) + (product(top, low) + product(rest, high))


def gather_pieces(received, held):
    parts, chunk = received.shape[0], held.shape[0]
    width = received.shape[2] // chunk
    for s in range(chunk):
        for p in range(parts):
            held[s, :, p * width : (p + 1) * width] = received[p, :, s * width : (s + 1) * width]


def scatter_pieces(held, sent):
    parts, chunk = sent.shape[0], held.shape[0]
    width = sent.shape[2] // chunk
    for s in range(chunk):
        for p in range(parts):
            sent[p, :, s * width : (s + 1) * width] = held[s, :, p * width : (p + 1) * width]


def assemble_kernel(received, matrix, out, held):
    gather_pieces(received, held)
    chunk, k, length = held.shape
    product = split_product(held[...].reshape(chunk * k, length), matrix[...])
    out[...] = product.reshape(out.shape)


def chunk_of(spectators, width, k):
    for chunk in range(1, spectators):
        if spectators % chunk == 0 and chunk * width % 128 == 0 and chunk * k >= 256:
            return chunk
    return spectators


def assemble(received, spectators, matrix):
    parts, k, area = received.shape
    chunk = chunk_of(spectators, area // spectators, k)
    length, points = matrix.shape
    if k % 8:
        held = received.reshape(parts, k, spectators, -1).transpose(2, 1, 0, 3)
        return apply(held.reshape(spectators, k, length), matrix)
    return pl.pallas_call(
        assemble_kernel,
        grid=(spectators // chunk,),
        in_specs=[
            pl.BlockSpec((parts, k, area // spectators * chunk), lambda i: (0, 0, i)),
            pl.BlockSpec((length, points), lambda i: (0, 0)),
        ],
        out_specs=pl.BlockSpec((chunk, k, points), lambda i: (i, 0, 0)),
        out_shape=jax.ShapeDtypeStruct((spectators, k, points), jnp.float32),
        scratch_shapes=[pltpu.VMEM((chunk, k, length), jnp.float32)],
    )(received, matrix)


def halves(values):
    high = values.astype(jnp.bfloat16)
    return high, (values - high.astype(jnp.float32)).astype(jnp.bfloat16)


def product_of(left, right):
    product = functools.partial(jnp.dot, preferred_element_type=jnp.float32)
    return product(left[0], right[0]) + (product(left[0], right[1]) + product(left[1], right[0]))


def planes_kernel(flows, sizes, chunks, volume, *refs):
    row, col = lax.axis_index("rows"), lax.axis_index("cols")

    def place(axis, index):
        return (index, col) if axis == "rows" else (row, index)

    matrix = refs[0]
    inputs = [refs[1 + 4 * i : 5 + 4 * i] for i in range(len(flows))]
    at = 1 + 4 * len(flows)
    outs = refs[at : at + len(flows)]
    at += len(flows)
    high, low = refs[at : at + 2]
    at += 2
    buffers = [refs[at + 9 * i : at + 9 * i + 9] for i in range(len(flows))]

    barrier = pltpu.get_barrier_semaphore()
    waits = 0
    for axis in sorted(set(axis for axis, _ in flows)):
        size = sizes[axis]
        me = lax.axis_index(axis)
        for step in range(1, size):
            peer = lax.rem(me + step, size)
            pl.semaphore_signal(barrier, inc=1, device_id=place(axis, peer), device_id_type=MESH)
        waits += size - 1
    high[...], low[...] = halves(matrix[...])
    pl.semaphore_wait(barrier, waits)

    def copies(flow, turn, c):
        axis, _ = flows[flow]
        size = sizes[axis]
        me = lax.axis_index(axis)
        sent, received = buffers[flow][2 * turn : 2 * turn + 2]
        send_sem, recv_sem = buffers[flow][4 + 2 * turn : 6 + 2 * turn]
        order = sorted(range(1, size), key=lambda step: abs(2 * step - size))
        for step in order:
            peer = lax.rem(me + step, size)
            yield pltpu.make_async_remote_copy(
                src_ref=sent.at[c, peer],
                dst_ref=received.at[c, me],
                send_sem=send_sem.at[c, step],
                recv_sem=recv_sem.at[c, step],
                device_id=place(axis, peer),
                device_id_type=MESH,
            )

    def launch(flow, turn, c):
        me = lax.axis_index(flows[flow][0])
        for copy in copies(flow, turn, c):
            copy.start()
        sent, received = buffers[flow][2 * turn : 2 * turn + 2]
        received[c, me] = sent[c, me]

    def lanes(area, c):
        if chunks == 1:
            return slice(None)
        return pl.ds(pl.multiple_of(c * (area // chunks), 128), area // chunks)

    def first(c, carry):
        for flow in range(len(flows)):
            source, sent = inputs[flow][0], buffers[flow][0]
            part = source[:, :, lanes(source.shape[2], c)]
            part = part.reshape(matrix.shape[0], part.shape[2])
            product = product_of((high[...], low[...]), halves(part))
            sent[c] = product.reshape(sent.shape[1:])
            launch(flow, 0, c)
        return carry

    def second(c, carry):
        for flow in range(len(flows)):
            _, sq_s, sq_k, sq_l = inputs[flow]
            vertical = flows[flow][1]
            held = buffers[flow][8]
            chunk, k, length = held.shape
            for copy in copies(flow, 0, c):
                copy.wait_recv()
            gather_pieces(buffers[flow][1].at[c], held)
            both = (high[...], low[...])
            values = product_of(halves(held[...].reshape(chunk * k, length)), both)
            parts = [sq_s[pl.ds(c * chunk, chunk)], sq_k[...][None], sq_l[...][None]]
            parts = [jnp.broadcast_to(part, held.shape) for part in parts]
            squares = parts[0] + parts[1] + parts[2]
            nonzero = jnp.where(squares > 0, squares, 1.0)
            weights = jnp.where(
                squares > 0, DIPOLE_STRENGTH * (3.0 * parts[vertical] - squares) / nonzero, 0.0
            )
            values = values * (weights / volume).reshape(chunk * k, length)
            held[...] = product_of(halves(values), both).reshape(held.shape)
            scatter_pieces(held, buffers[flow][2].at[c])
            launch(flow, 1, c)
        return carry

    def third(c, carry):
        for flow in range(len(flows)):
            for copy in copies(flow, 1, c):
                copy.wait_recv()
            received, out = buffers[flow][3], outs[flow]
            part = received[c].reshape(matrix.shape[0], received.shape[3])
            product = product_of((high[...], low[...]), halves(part))
            out[:, lanes(out.shape[1], c)] = product
            for turn in range(2):
                for copy in copies(flow, turn, c):
                    copy.wait_send()
        return carry

    for stage in (first, second, third):
        lax.fori_loop(0, chunks, stage, 0)


def planes(exchange, flows, matrix):
    sizes = exchange.sizes
    length = matrix.shape[0]
    counts = []
    for axis, _, received, sq_s, sq_k, _ in flows:
        spectators = sq_s.shape[0]
        width = received.shape[2] // spectators
        counts.append(spectators // chunk_of(spectators, width, sq_k.shape[0]))
    chunks = counts[0] if len(set(counts)) == 1 else 1
    operands, outs, scratch = [matrix], [], []
    scratch += [pltpu.VMEM((length, length), jnp.bfloat16)] * 2
    for axis, _, received, sq_s, sq_k, sq_l in flows:
        operands += [received, sq_s[:, None, None], sq_k[:, None], sq_l[None, :]]
        area, k, size = received.shape[2], sq_k.shape[0], sizes[axis]
        outs.append(jax.ShapeDtypeStruct((length, area), jnp.float32))
        scratch += [pltpu.VMEM((chunks, size, k, area // chunks), jnp.float32)] * 4
        scratch += [pltpu.SemaphoreType.DMA((chunks, size))] * 4
        scratch += [pltpu.VMEM((sq_s.shape[0] // chunks, k, length), jnp.float32)]
    exchange.calls += 1
    vmem = pl.BlockSpec(memory_space=pltpu.VMEM)
    return pl.pallas_call(
        functools.partial(
            planes_kernel,
            tuple((flow[0], flow[1]) for flow in flows),
            sizes,
            chunks,
            float(length) ** 3,
        ),
        out_shape=outs,
        in_specs=[vmem] * len(operands),
        out_specs=[vmem] * len(outs),
        scratch_shapes=scratch,
        compiler_params=pltpu.CompilerParams(
            collective_id=exchange.calls - 1,
            has_side_effects=True,
            vmem_limit_bytes=60 * 1024 * 1024,
        ),
        name=f"planes_{exchange.calls - 1}",
    )(*operands)


def blocks(turned, parts):
    first, length, last = turned.shape
    turned = turned.reshape(first, parts, length // parts, last).transpose(1, 0, 2, 3)
    return turned.reshape(parts, first, length // parts * last)


def product_blocks(matrix, received, parts):
    turned = jnp.dot(matrix, received.reshape(-1, received.shape[2]), precision=HIGH)
    return turned.reshape(parts, turned.shape[0] // parts, turned.shape[1])


def per_device(sizes, wave_coarse, potential_coarse, potential_fine):
    row, col = lax.axis_index("rows"), lax.axis_index("cols")
    rows, cols = sizes["rows"], sizes["cols"]
    nc, nf = wave_coarse.shape[2], potential_fine.shape[2]
    exchange = Exchanger(sizes)

    coarse_matrix = cas_matrix(nc)
    fine_matrix = cas_matrix(nf)
    decay = jnp.exp(-0.5 * TIME_STEP * wavenumbers(nc, nc, 0, 2.0) ** 2)[:, None] / nc
    evolve = jnp.dot(coarse_matrix, decay * coarse_matrix, precision=HIGHEST)
    lift = jnp.dot(coarse_matrix, decay * lift_matrix(nc), precision=HIGHEST)

    xr = yr = nc // rows
    spectators = nc // cols
    turned = jnp.einsum("xyz,zk->ykx", wave_coarse, evolve, precision=HIGH)
    (got,) = exchange((blocks(turned, cols), "cols"))
    (got,) = exchange((product_blocks(evolve.T, got, rows), "rows"))
    evolved = assemble(got, spectators, evolve)
    turned = jnp.einsum("zyx,xk->zky", evolved * evolved, coarse_matrix, precision=HIGH)
    got, back = exchange(
        (blocks(turned, cols), "cols"), (give(evolved.transpose(1, 0, 2), None, rows), "rows")
    )
    back = take(back, "rows", yr)
    got, back = exchange(
        (product_blocks(coarse_matrix, got, rows), "rows"), (give(back, None, cols), "cols")
    )
    spectrum, evolved = assemble(got, spectators, coarse_matrix), take(back, "cols", xr)
    z_block, x_block = nc // rows, nc // cols
    weights = dipolar_weights(
        wavenumbers(nc, x_block, col * x_block, 2.0)[:, None, None] ** 2,
        wavenumbers(nc, nc, 0, 2.0)[None, None, :] ** 2,
        wavenumbers(nc, z_block, row * z_block, 2.0)[None, :, None] ** 2,
        nc,
    )
    turned = jnp.einsum("xzy,yk->xkz", weights * spectrum, coarse_matrix, precision=HIGH)
    (got,) = exchange((blocks(turned, cols), "cols"))
    (got,) = exchange((product_blocks(coarse_matrix, got, rows), "rows"))
    field_dd = assemble(got, spectators, coarse_matrix).transpose(1, 0, 2)
    density = evolved * evolved
    damped = jnp.exp(-TIME_STEP * (potential_coarse + CONTACT * density + field_dd)) * evolved
    partial_sum = jnp.sum(damped * damped)

    got, sums = exchange(
        (blocks(jnp.einsum("xyz,zk->ykx", damped, lift, precision=HIGH), cols), "cols"),
        (jnp.full((cols, 8, 128), partial_sum, jnp.float32), "cols"),
    )
    partial_sum = jnp.sum(sums[:, 0, 0])
    got, sums = exchange(
        (product_blocks(lift.T, got, rows), "rows"),
        (jnp.full((rows, 8, 128), partial_sum, jnp.float32), "rows"),
    )
    scale = lax.rsqrt(jnp.sum(sums[:, 0, 0]) / float(nc) ** 3 + EPSILON)
    evolved = assemble(got, nf // cols, lift) * scale

    density = evolved * evolved
    half = nf // 2
    near, far = fine_matrix[:, :half], fine_matrix[:, half:]
    got_near, got_far = exchange(
        (blocks(jnp.einsum("zyx,xk->ykz", density, near, precision=HIGH), rows), "rows"),
        (blocks(jnp.einsum("zyx,xk->zky", density, far, precision=HIGH), cols), "cols"),
    )
    y_block, z_block = nf // cols, nf // rows
    near_block, far_block = half // rows, half // cols
    every = wavenumbers(nf, nf, 0, 1.0) ** 2
    near_flow = (
        "cols",
        2,
        got_near,
        wavenumbers(nf, near_block, row * near_block, 1.0) ** 2,
        wavenumbers(nf, y_block, col * y_block, 1.0) ** 2,
        every,
    )
    far_flow = (
        "rows",
        1,
        got_far,
        wavenumbers(nf, far_block, half + col * far_block, 1.0) ** 2,
        wavenumbers(nf, z_block, row * z_block, 1.0) ** 2,
        every,
    )
    got_far, got_near = planes(exchange, (far_flow, near_flow), fine_matrix)
    got_near, got_far = exchange(
        (got_near.reshape(rows, nf // rows, -1), "rows"),
        (got_far.reshape(cols, nf // cols, -1), "cols"),
    )
    z_extent, y_extent = nf // cols, nf // rows
    near_field = got_near.reshape(rows, y_extent, near_block, z_extent)
    near_field = near_field.transpose(3, 1, 0, 2).reshape(z_extent, y_extent, half)
    far_field = got_far.reshape(cols, z_extent, far_block, y_extent)
    far_field = far_field.transpose(1, 3, 0, 2).reshape(z_extent, y_extent, half)
    spectrum = jnp.concatenate([near_field, far_field], axis=2)
    field_dd = jnp.einsum("zyk,kx->zyx", spectrum, fine_matrix, precision=HIGH)
    damped = jnp.exp(-TIME_STEP * (potential_fine + CONTACT * density + field_dd)) * evolved
    total = jnp.sum(damped * damped)
    for axis in ("rows", "cols"):
        (sums,) = exchange((jnp.full((sizes[axis], 8, 128), total, jnp.float32), axis))
        total = jnp.sum(sums[:, 0, 0])
    return damped * lax.rsqrt(total / float(nf) ** 3 + EPSILON)


def solution(mesh):
    sizes = {"rows": mesh.shape["rows"], "cols": mesh.shape["cols"]}
    placed = (P("rows", "cols", None), P("rows", "cols", None), P("cols", "rows", None))
    return jax.shard_map(
        functools.partial(per_device, sizes),
        mesh=mesh,
        in_specs=placed,
        out_specs=P("cols", "rows", None),
        check_vma=False,
    )
```
